256 devices in a mesh: gx: 32 (over x_lo, z, core), gy: 8 (over x_hi, y).
Axes of the slice: x: 4 (x_hi: 2, x_lo: 2; x = x_hi * 2 + x_lo), y: 4, z: 8, core: 2. Of those that a mesh axis runs over, the one named last changes fastest.
Arguments:
- temp_adjoint: float32 [8, 1024, 4096], P(None, 'gy', 'gx'), may hold values from -6 to 6
- height_adjoint: float32 [1024, 4096], P('gy', 'gx'), may hold values from -6 to 6
- east_velocity: float32 [8, 1024, 4096], P(None, 'gy', 'gx'), may hold values from -0.8 to 0.8
- north_velocity: float32 [8, 1024, 4096], P(None, 'gy', 'gx'), may hold values from -0.8 to 0.8
- temp_store: float32 [8, 1024, 4096], P(None, 'gy', 'gx'), may hold values from -4 to 4
- salt_store: float32 [8, 1024, 4096], P(None, 'gy', 'gx'), may hold values from -4 to 4
- slot_map: int32 [32, 8, 8], P('gx', 'gy'), may hold values from 0 to 7, each once within a row
- land_mask: int32 [8, 1024, 4096], P(None, 'gy', 'gx'), may hold values 0 or 1
- ocean_depth: float32 [1024, 4096], P('gy', 'gx'), may hold values from 0.1 to 1
Outputs:
- temp_back: float32 [8, 1024, 4096], P(None, 'gy', 'gx')
- salt_back: float32 [8, 1024, 4096], P(None, 'gy', 'gx')
- surface_adjoint: float32 [1024, 4096], P('gy', 'gx')
The draws below stay inside these ranges and needn't reach their ends.
Inputs may be any that keep to these rules, and one draw needn't show every extreme that they name: `slot_map`: each tile's entries over the last dimension name every slot 0 to 7 once.
All inputs are finite; a program needn't handle non-finite values. No bound on the sum of `land_mask` on one device may be relied on, other than what follows from the above.
Results may differ from the reference program's by a relative error of at most 0.00013.
Values sent between devices are 32-bit elements; how exact they have to be, the bound alone decides.
A program may use at most 64 MiB of HBM per device.

```python
import math
import jax
import jax.numpy as jnp
from jax import lax

LEV = 8
CY = 128
CX = 128
ITERS = 6
TILES_X = 32
TILES_Y = 8
NX = 4096
NY = 1024


def plant(drawn, rng, least, top_value):
    index_at = [jax.random.randint(jax.random.fold_in(rng, axis), (), 0, length) for axis, length in enumerate(drawn.shape)]
    main_axis = drawn.shape.index(max(drawn.shape))
    beside = index_at[:main_axis] + [(index_at[main_axis] + 1) % drawn.shape[main_axis]] + index_at[main_axis + 1:]
    return drawn.at[tuple(index_at)].set(least).at[tuple(beside)].set(top_value)


def level_of(rng, extent, split, smallest, top_value):
    gain, own = 1.0, jax.random.fold_in(rng, 6)
    for dim, shards_of in split:
        draws = jnp.exp(jax.random.uniform(jax.random.fold_in(own, dim), (shards_of,), jnp.float32, smallest / len(split), top_value / len(split)))
        gain = gain * jnp.repeat(draws, extent[dim] // shards_of).reshape([-1 if axis == dim else 1 for axis in range(len(extent))])
    return gain


def bell_draw(key, shape, width, reach, shards=(), kind=jnp.bfloat16):
    array = width * jax.random.normal(key, shape, jnp.float32)
    if shards:
        array = array * level_of(key, shape, shards, -0.22, 0.18)
    return jnp.clip(array, -reach, reach).astype(kind)


def setup_inputs(seed: int = 0) -> dict:
    key_list = jax.random.split(jax.random.key(seed), 10)
    temp_adjoint = bell_draw(key_list[0], (LEV, NY, NX), 1.0, 6.0, ((1, 8), (2, 32)), jnp.float32)
    height_adjoint = bell_draw(key_list[1], (NY, NX), 1.0, 6.0, ((0, 8), (1, 32)), jnp.float32)
    east_velocity = bell_draw(key_list[2], (LEV, NY, NX), 0.2, 0.8, ((1, 8), (2, 32)), jnp.float32)
    north_velocity = bell_draw(key_list[3], (LEV, NY, NX), 0.2, 0.8, ((1, 8), (2, 32)), jnp.float32)
    temp_store = bell_draw(key_list[4], (LEV, NY, NX), 1.0, 4.0, ((1, 8), (2, 32)), jnp.float32)
    salt_store = bell_draw(key_list[5], (LEV, NY, NX), 1.0, 4.0, ((1, 8), (2, 32)), jnp.float32)
    slot_map = jax.vmap(lambda own: jax.random.permutation(own, LEV))(jax.random.split(key_list[6], TILES_X * TILES_Y)).reshape((TILES_X, TILES_Y, LEV)).astype(jnp.int32)
    land_mask = plant((jax.random.randint(key_list[7], (LEV, NY, NX), 0, 4) < 3).astype(jnp.int32), jax.random.fold_in(key_list[7], 1), 0, 1)
    ocean_depth = jnp.clip(jnp.exp(math.log(1.0) - 2.3025851 * jax.random.uniform(key_list[8], (NY, NX), jnp.float32) ** level_of(key_list[8], (NY, NX), ((0, 8), (1, 32)), -0.2, 0.2)), 0.1, 1.0)
    return dict(temp_adjoint=temp_adjoint, height_adjoint=height_adjoint, east_velocity=east_velocity, north_velocity=north_velocity, temp_store=temp_store, salt_store=salt_store, slot_map=slot_map, land_mask=land_mask, ocean_depth=ocean_depth)


DIFFUSE = 0.2
TIMESTEP = 1.0
STIFFNESS = 8.0
GRAVITY = 4.0
THERMAL = 0.5
NONLINEAR = 0.4
CABBELING = 0.3
HALINE = 0.8


def west_of(grid_field):
    return jnp.roll(grid_field, 1, axis=-1)


def east_of(grid_field):
    return jnp.roll(grid_field, -1, axis=-1)


def south_of(grid_field):
    zero_edge = jnp.zeros_like(grid_field[..., :1, :])
    return jnp.concatenate([zero_edge, grid_field[..., :-1, :]], axis=-2)


def north_of(grid_field):
    zero_edge = jnp.zeros_like(grid_field[..., :1, :])
    return jnp.concatenate([grid_field[..., 1:, :], zero_edge], axis=-2)


NEIGHBOURS = (west_of, east_of, south_of, north_of)


def surface_apply(grid_field, face_links, face_weights):
    applied = grid_field
    for neighbour, face_weight in zip(NEIGHBOURS, face_weights):
        applied = applied + face_weight * (grid_field - neighbour(grid_field))
    return applied


def reference(temp_adjoint, height_adjoint, east_velocity, north_velocity, temp_store, salt_store, slot_map, land_mask, ocean_depth):
    wet_cells = land_mask.astype(jnp.float32)
    masked = wet_cells * temp_adjoint
    east_coef = DIFFUSE - 0.5 * east_velocity
    west_coef = DIFFUSE + 0.5 * east_velocity
    north_coef = DIFFUSE - 0.5 * north_velocity
    south_coef = DIFFUSE + 0.5 * north_velocity
    inflow = west_of(east_coef * masked) + east_of(west_coef * masked)
    inflow = inflow + south_of(north_coef * masked) + north_of(south_coef * masked)
    tracer_back = masked + TIMESTEP * (inflow - (east_coef + west_coef + north_coef + south_coef) * masked)

    open_cells = wet_cells[0]
    face_links = [open_cells * neighbour(open_cells) for neighbour in NEIGHBOURS]
    face_weights = [STIFFNESS * 0.5 * (ocean_depth + neighbour(ocean_depth)) * link_open
                    for neighbour, link_open in zip(NEIGHBOURS, face_links)]
    target = open_cells * height_adjoint
    solution = jnp.zeros_like(target)
    residual = target
    direction = target
    norm_now = jnp.sum(residual * residual)
    for iteration in range(ITERS):
        image_field = surface_apply(direction, face_links, face_weights)
        step_size = norm_now / jnp.sum(direction * image_field)
        solution = solution + step_size * direction
        residual = residual - step_size * image_field
        norm_next = jnp.sum(residual * residual)
        direction = residual + (norm_next / norm_now) * direction
        norm_now = norm_next

    height_load = ocean_depth * solution
    pressure_pull = jnp.zeros_like(height_load)
    for neighbour, link_open in zip(NEIGHBOURS, face_links):
        pressure_pull = pressure_pull + link_open * (neighbour(height_load) - height_load)
    adj_pressure = -GRAVITY * pressure_pull
    thickness = 1.0 + jnp.arange(LEV, dtype=jnp.float32) / LEV
    adj_density = thickness[:, None, None] * adj_pressure[None] * wet_cells

    slot_onehot = (slot_map[:, :, :, None] == jnp.arange(LEV, dtype=jnp.int32)[None, None, None, :]).astype(jnp.float32)
    tiles_x = slot_map.shape[0]
    tiles_y = slot_map.shape[1]

    def reorder(store):
        blocks = store.reshape(LEV, tiles_y, CY, tiles_x, CX)
        ordered = jnp.einsum("ijks,sjyix->kjyix", slot_onehot, blocks, precision=lax.Precision.HIGHEST)
        return jnp.roll(ordered.reshape(LEV, NY, NX), -(NX // 2), axis=-1)

    ck_temp = reorder(temp_store)
    ck_salt = reorder(salt_store)
    temp_back = tracer_back + (THERMAL + 2.0 * NONLINEAR * ck_temp + CABBELING * ck_salt) * adj_density
    salt_back = (HALINE + CABBELING * ck_temp) * adj_density
    return temp_back, salt_back, solution
```

```python
import itertools
import functools

import jax
import jax.numpy as jnp
from jax import lax
from jax.experimental import pallas as pl
from jax.experimental.pallas import tpu as pltpu
from jax.sharding import PartitionSpec as P

DIFFUSE = 0.2
TIMESTEP = 1.0
STIFFNESS = 8.0
GRAVITY = 4.0
THERMAL = 0.5
NONLINEAR = 0.4
CABBELING = 0.3
HALINE = 0.8
ITERS = 6
SCALE = 16.0
G = 8
LEV, CY, CX = 8, 128, 128
ROWS, COLS = CY + 2 * G, 2 * CX
SIZES = {"xl": 2, "z": 8, "c": 2, "xh": 2, "y": 4}
STAGES = (("z", "c"), ("xl", "xh", "y"))
F32 = jnp.float32


def two_sum(a, b):
    s = a + b
    t = s - a
    return s, (a - (s - t)) + (b - t)


def quick(a, b):
    s = a + b
    return s, b - (s - a)


def df_add(x, y):
    s, e = two_sum(x[0], y[0])
    return quick(s, e + (x[1] + y[1]))


def df_neg(x):
    return -x[0], -x[1]


def halves(a):
    c = 4097.0 * a
    hi = c - (c - a)
    return hi, a - hi


def two_prod(a, b):
    p = a * b
    ah, al = halves(a)
    bh, bl = halves(b)
    return p, ((ah * bh - p) + ah * bl + al * bh) + al * bl


def df_mul(x, y):
    p, e = two_prod(x[0], y[0])
    return quick(p, e + (x[0] * y[1] + x[1] * y[0]))


def df_div(x, y):
    q = x[0] / y[0]
    p, e = two_prod(q, y[0])
    s, t = two_sum(x[0], -p)
    r = s + (t + (x[1] - (e + q * y[1])))
    return quick(q, r / y[0])


def peers(stage):
    return [o for o in itertools.product(*[range(SIZES[d]) for d in stage]) if any(o)]


def tree(x):
    while x.shape[0] > 8:
        h = x.shape[0] // 2
        x = x[:h] + x[h:]
    return x


def kernel(
    slot_ref, ta_h, ha_h, ev_h, nv_h, ts_h, ss_h, lm_h, od_h,
    tb_h, sb_h, sa_h,
    ta, ha, ev, nv, store, lm, od,
    stage, fetched, back, out, edge, edge_in, rows_out, rows_in, corner_in,
    zed, zed_in, zrow, zrow_in, field, depth, wgt, basis, mail, mail_in, sol,
    load_sem, bulk_sem, halo_sem, zed_sem, mail_sem, out_sem,
):
    gx, gy = lax.axis_index("gx"), lax.axis_index("gy")
    co = {"xl": gx // 16, "z": (gx // 2) % 8, "c": gx % 2, "xh": gy // 4, "y": gy % 4}

    def peer(st, off):
        n = dict(co)
        for d, o in zip(st, off):
            n[d] = (co[d] + o) % SIZES[d]
        return (n["xl"] * 16 + n["z"] * 2 + n["c"], n["xh"] * 4 + n["y"])

    west, east = (gx + 31) % 32, (gx + 1) % 32
    south, north = (gy + 7) % 8, (gy + 1) % 8
    partner = ((gx + 16) % 32, gy)

    local = [
        (od_h, od), (lm_h.at[0], lm.at[0]), (ha_h, ha),
        (ts_h, store.at[0]), (ss_h, store.at[1]),
        (lm_h.at[pl.ds(1, LEV - 1)], lm.at[pl.ds(1, LEV - 1)]),
        (ta_h, ta), (ev_h, ev), (nv_h, nv),
    ]
    loads = [pltpu.make_async_copy(a, b, load_sem.at[i]) for i, (a, b) in enumerate(local)]
    for c in loads:
        c.start()

    barrier = pltpu.get_barrier_semaphore()
    greeted = [peer(st, off) for st in STAGES for off in peers(st)]
    greeted += [(a, b) for a in (west, east) for b in (south, gy, north)]
    for who in greeted:
        pl.semaphore_signal(barrier, inc=1, device_id=who)

    lane = lax.broadcasted_iota(jnp.int32, (CY, CX), 1)
    row = lax.broadcasted_iota(jnp.int32, (CY, CX), 0)
    lane8 = lane[:8]

    for c in loads[:3]:
        c.wait()
    opened = lm[0].astype(F32)
    target = opened * ha[...]
    dm = opened * od[...]
    field[pl.ds(G, CY), pl.ds(0, CX)] = target
    depth[pl.ds(G, CY), pl.ds(0, CX)] = dm
    edge[...] = jnp.where(
        (lane < 8) | (lane >= 120),
        target,
        jnp.where(lane < 64, pltpu.roll(dm, 8, 1), pltpu.roll(dm, 120, 1)),
    )
    rows_out[0, 0] = target[:8]
    rows_out[0, 1] = dm[:8]
    rows_out[1, 0] = target[120:]
    rows_out[1, 1] = dm[120:]

    for c in loads[3:5]:
        c.wait()
    for k in range(LEV):
        slot = slot_ref[0, 0, k]
        stage[0, k] = store[0, slot]
        stage[1, k] = store[1, slot]

    pl.semaphore_wait(barrier, len(greeted))

    low, high = pl.ds(0, 8), pl.ds(120, 8)
    halo = [
        (edge, edge_in.at[0], (west, gy)),
        (edge, edge_in.at[1], (east, gy)),
        (rows_out.at[0], rows_in.at[0], (gx, south)),
        (rows_out.at[1], rows_in.at[1], (gx, north)),
        (edge.at[low], corner_in.at[0], (west, south)),
        (edge.at[low], corner_in.at[1], (east, south)),
        (edge.at[high], corner_in.at[2], (west, north)),
        (edge.at[high], corner_in.at[3], (east, north)),
    ]
    halos = []
    for i, (a, b, who) in enumerate(halo):
        c = pltpu.make_async_remote_copy(a, b, halo_sem.at[0, i], halo_sem.at[1, i], device_id=who)
        c.start()
        halos.append(c)
    bulks = []
    for k in range(LEV):
        c = pltpu.make_async_remote_copy(
            stage.at[:, k], fetched.at[:, k], bulk_sem.at[0, k], bulk_sem.at[1, k], device_id=partner
        )
        c.start()
        bulks.append(c)

    for c in halos:
        c.wait_recv()
    has_north = jnp.where(gy < 7, 1.0, 0.0).astype(F32)
    has_south = jnp.where(gy > 0, 1.0, 0.0).astype(F32)

    def side(east_tile, west_tile, lanes):
        got = jnp.where(lanes < 64, east_tile, west_tile)
        n = got.shape[0]
        inner = jnp.where(lanes < 64, pltpu.roll(got, 120, 1), pltpu.roll(got, 8, 1))
        return got, inner

    mid, top, bottom = pl.ds(G, CY), pl.ds(G + CY, G), pl.ds(0, G)
    own, far = pl.ds(0, CX), pl.ds(CX, CX)
    a, b = side(edge_in[0], edge_in[1], lane)
    field[mid, far] = a
    depth[mid, far] = b
    a, b = side(corner_in[0], corner_in[1], lane8)
    field[top, far] = a * has_north
    depth[top, far] = b * has_north
    a, b = side(corner_in[2], corner_in[3], lane8)
    field[bottom, far] = a * has_south
    depth[bottom, far] = b * has_south
    field[top, own] = rows_in[0, 0] * has_north
    depth[top, own] = rows_in[0, 1] * has_north
    field[bottom, own] = rows_in[1, 0] * has_south
    depth[bottom, own] = rows_in[1, 1] * has_south

    d = depth[...]
    for i, (shift, axis) in enumerate(((1, 1), (COLS - 1, 1), (1, 0), (ROWS - 1, 0))):
        e = pltpu.roll(d, shift, axis)
        wgt[i] = jnp.where((d > 0.0) & (e > 0.0), (STIFFNESS * 0.5 / SCALE) * (d + e), 0.0)

    def apply(v):
        return (
            wgt[0] * (v - pltpu.roll(v, 1, 1))
            + wgt[1] * (v - pltpu.roll(v, COLS - 1, 1))
            + wgt[2] * (v - pltpu.roll(v, 1, 0))
            + wgt[3] * (v - pltpu.roll(v, ROWS - 1, 0))
        )

    partial = []
    v = field[...]
    for k in range(ITERS):
        nxt = apply(v)
        if k == 0:
            basis[...] = nxt
        here, there = v[G : G + CY, :CX], nxt[G : G + CY, :CX]
        partial.append(tree(here * here))
        partial.append(tree(here * there))
        v = nxt
    nm = len(partial)
    hi = jnp.stack(partial)
    lo = jnp.zeros_like(hi)
    for s in (4, 2, 1):
        hi, lo = df_add((hi, lo), (pltpu.roll(hi, s, 1), pltpu.roll(lo, s, 1)))
    sub8 = lax.broadcasted_iota(jnp.int32, (8, CX), 0)

    def packed(x):
        done = []
        for first in (0, 8):
            t = jnp.zeros((8, CX), F32)
            for j in range(first, min(first + 8, nm)):
                t = jnp.where(sub8 == j - first, x[j], t)
            done.append(t)
        return jnp.concatenate(done, axis=0)

    hi, lo = packed(hi), packed(lo)
    for s in (64, 32, 16, 8, 4, 2, 1):
        hi, lo = df_add((hi, lo), (pltpu.roll(hi, s, 1), pltpu.roll(lo, s, 1)))
    letter = jnp.where(
        lane8 < 64,
        jnp.where(lane8 < 32, hi[:8], hi[8:]),
        jnp.where(lane8 < 96, lo[:8], lo[8:]),
    )

    def post(st):
        mail[st] = letter
        for i, off in enumerate(peers(STAGES[st])):
            pltpu.make_async_remote_copy(
                mail.at[st], mail_in.at[st, i], mail_sem.at[0, st], mail_sem.at[1, st],
                device_id=peer(STAGES[st], off),
            ).start()

    def collect(st):
        pltpu.make_async_copy(mail_in.at[st], mail_in.at[st], mail_sem.at[1, st]).wait()
        his = [mail[st]] + [mail_in[st, i] for i in range(len(peers(STAGES[st])))]
        terms = [(t, pltpu.roll(t, 64, 1)) for t in his]
        while len(terms) > 1:
            terms = [df_add(terms[i], terms[i + 1]) for i in range(0, len(terms), 2)]
        return terms[0]

    post(0)

    for c in loads[5:]:
        c.wait()
    z = jnp.zeros((CY, CX), F32)
    zn = jnp.zeros((8, CX), F32)
    zs = jnp.zeros((8, CX), F32)
    for k in range(LEV):
        m = lm[k].astype(F32) * ta[k]
        ec = DIFFUSE - 0.5 * ev[k]
        wc = DIFFUSE + 0.5 * ev[k]
        nc = DIFFUSE - 0.5 * nv[k]
        sc = DIFFUSE + 0.5 * nv[k]
        ef, wf, nf, sf = ec * m, wc * m, nc * m, sc * m
        inflow = jnp.where(lane == 0, 0.0, pltpu.roll(ef, 1, 1))
        inflow = inflow + jnp.where(lane == CX - 1, 0.0, pltpu.roll(wf, CX - 1, 1))
        inflow = inflow + jnp.where(row == 0, 0.0, pltpu.roll(nf, 1, 0))
        inflow = inflow + jnp.where(row == CY - 1, 0.0, pltpu.roll(sf, CY - 1, 0))
        back[k] = m + TIMESTEP * (inflow - (ec + wc + nc + sc) * m)
        z = jnp.where(lane == k, pltpu.roll(wf, k, 1) if k else wf, z)
        z = jnp.where(lane == 120 + k, pltpu.roll(ef, 121 + k, 1) if k < 7 else ef, z)
        zrow[1, pl.ds(k, 1)] = nf[CY - 1 :]
        zrow[0, pl.ds(k, 1)] = sf[:1]
    zed[...] = z
    zeds = []
    for i, (a, b, who) in enumerate((
        (zed, zed_in.at[0], (west, gy)),
        (zed, zed_in.at[1], (east, gy)),
        (zrow.at[0], zrow_in.at[0], (gx, south)),
        (zrow.at[1], zrow_in.at[1], (gx, north)),
    )):
        c = pltpu.make_async_remote_copy(a, b, zed_sem.at[0, i], zed_sem.at[1, i], device_id=who)
        c.start()
        zeds.append(c)

    total = collect(0)
    letter = jnp.where(lane8 < 64, total[0], pltpu.roll(total[1], 64, 1))
    post(1)

    for c in zeds:
        c.wait_recv()
    ze, zw = zed_in[0], zed_in[1]
    for k in range(LEV):
        b = back[k]
        b = b + jnp.where(lane == 0, pltpu.roll(zw, 8 - k, 1), 0.0)
        b = b + jnp.where(lane == CX - 1, pltpu.roll(ze, 127 - k, 1), 0.0)
        b = b + jnp.where(row == 0, zrow_in[1, pl.ds(k, 1)] * has_south, 0.0)
        back[k] = b + jnp.where(row == CY - 1, zrow_in[0, pl.ds(k, 1)] * has_north, 0.0)

    total = collect(1)
    cur = tuple(jnp.concatenate([t, pltpu.roll(t, 96, 1)], axis=0) for t in total)
    prev = (jnp.zeros_like(cur[0]), jnp.zeros_like(cur[0]))

    def pick(x, k):
        return x[0][k : k + 1], x[1][k : k + 1]

    def spread(x):
        return jnp.broadcast_to(x[0], cur[0].shape), jnp.broadcast_to(x[1], cur[0].shape)

    def up(x):
        return pltpu.roll(x[0], 15, 0), pltpu.roll(x[1], 15, 0)

    norm = pick(cur, 0)
    ratio = df_div(pick(cur, 1), norm)
    ja, jb = [ratio], []
    for k in range(1, ITERS):
        nxt = df_add(up(cur), df_neg(df_mul(spread(ja[-1]), cur)))
        if k > 1:
            nxt = df_add(nxt, df_neg(df_mul(spread(jb[-1]), prev)))
        fresh = pick(nxt, k)
        new_ratio = df_div(pick(nxt, k + 1), fresh)
        ja.append(df_add(new_ratio, df_neg(ratio)))
        jb.append(df_div(fresh, norm))
        norm, ratio, prev, cur = fresh, new_ratio, cur, nxt
    steps, growths = [], []
    for k in range(ITERS):
        diag = 1.0 + SCALE * (ja[k][0] + ja[k][1])
        if k:
            off = (SCALE * SCALE) * (jb[k - 1][0] + jb[k - 1][1])
            growths.append(off * steps[-1] * steps[-1])
            diag = diag - off * steps[-1]
        steps.append(1.0 / diag)
    whole = (ROWS, COLS)
    steps = [jnp.broadcast_to(x[:1, :1], whole) for x in steps]
    growths = [jnp.broadcast_to(x[:1, :1], whole) for x in growths]

    r = field[...]
    p = r
    s = jnp.zeros_like(r)
    for k in range(ITERS):
        s = s + steps[k] * p
        if k + 1 < ITERS:
            q = p + SCALE * (basis[...] if k == 0 else apply(p))
            r = r - steps[k] * q
            p = r + growths[k] * p
    load = depth[...] * s
    pull = jnp.zeros_like(load)
    for i, (shift, axis) in enumerate(((1, 1), (COLS - 1, 1), (1, 0), (ROWS - 1, 0))):
        pull = pull + jnp.where(wgt[i] > 0.0, pltpu.roll(load, shift, axis) - load, 0.0)
    sol[...] = s[G : G + CY, :CX]
    sol_copy = pltpu.make_async_copy(sol, sa_h, out_sem.at[2, 0])
    sol_copy.start()
    pressure = -GRAVITY * pull[G : G + CY, :CX]

    outs = []
    for k in range(LEV):
        bulks[k].wait_recv()
        dens = ((1.0 + k / LEV) * pressure) * lm[k].astype(F32)
        ct, cs = fetched[0, k], fetched[1, k]
        out[0, k] = back[k] + (THERMAL + 2.0 * NONLINEAR * ct + CABBELING * cs) * dens
        out[1, k] = (HALINE + CABBELING * ct) * dens
        for i, dst in enumerate((tb_h, sb_h)):
            c = pltpu.make_async_copy(out.at[i, k], dst.at[k], out_sem.at[i, k])
            c.start()
            outs.append(c)
    for c in halos + bulks + zeds:
        c.wait_send()
    for st in range(2):
        pltpu.make_async_copy(mail_in.at[st], mail_in.at[st], mail_sem.at[0, st]).wait()
    sol_copy.wait()
    for c in outs:
        c.wait()


def body(ta, ha, ev, nv, ts, ss, slots, lm, od):
    vm = lambda *shape: pltpu.VMEM(shape, F32)
    cube = (LEV, CY, CX)
    dma = lambda *shape: pltpu.SemaphoreType.DMA(shape)
    n = len(peers(STAGES[0]))
    hbm = pl.BlockSpec(memory_space=pl.ANY)
    return pl.pallas_call(
        kernel,
        out_shape=(
            jax.ShapeDtypeStruct(cube, F32),
            jax.ShapeDtypeStruct(cube, F32),
            jax.ShapeDtypeStruct((CY, CX), F32),
        ),
        in_specs=[pl.BlockSpec(memory_space=pltpu.SMEM)] + [hbm] * 8,
        out_specs=(hbm, hbm, hbm),
        scratch_shapes=[
            vm(*cube), vm(CY, CX), vm(*cube), vm(*cube), vm(2, *cube), pltpu.VMEM(cube, jnp.int32), vm(CY, CX),
            vm(2, *cube), vm(2, *cube), vm(*cube), vm(2, *cube),
            vm(CY, CX), vm(2, CY, CX), vm(2, 2, 8, CX), vm(2, 2, 8, CX), vm(4, 8, CX),
            vm(CY, CX), vm(2, CY, CX), vm(2, 8, CX), vm(2, 8, CX),
            vm(ROWS, COLS), vm(ROWS, COLS), vm(4, ROWS, COLS), vm(ROWS, COLS),
            vm(2, 8, CX), vm(2, n, 8, CX), vm(CY, CX),
            dma(9), dma(2, LEV), dma(2, 8), dma(2, 4), dma(2, 2), dma(3, LEV),
        ],
        compiler_params=pltpu.CompilerParams(
            collective_id=0, has_side_effects=True, vmem_limit_bytes=40 << 20
        ),
        cost_estimate=pl.CostEstimate(flops=20000000, bytes_accessed=5000000, transcendentals=0),
        name="adjoint",
    )(slots, ta, ha, ev, nv, ts, ss, lm, od)


def solution(mesh):
    cube, flat = P(None, "gy", "gx"), P("gy", "gx")
    return jax.shard_map(
        body,
        mesh=mesh,
        in_specs=(cube, flat, cube, cube, cube, cube, P("gx", "gy", None), cube, flat),
        out_specs=(cube, cube, flat),
        check_vma=False,
    )
```

```python
import itertools
import functools

import jax
import jax.numpy as jnp
from jax import lax
from jax.experimental import pallas as pl
from jax.experimental.pallas import tpu as pltpu
from jax.sharding import PartitionSpec as P

DIFFUSE = 0.2
TIMESTEP = 1.0
STIFFNESS = 8.0
GRAVITY = 4.0
THERMAL = 0.5
NONLINEAR = 0.4
CABBELING = 0.3
HALINE = 0.8
ITERS = 6
SPAN = 8.0
G = 8
FIRST = 6
LEV, CY, CX = 8, 128, 128
ROWS, COLS = CY + 2 * G, 2 * CX
SIZES = {"xl": 2, "z": 8, "c": 2, "xh": 2, "y": 4}
STAGES = (("z", "c"), ("xl", "xh", "y"))
F32 = jnp.float32


def two_sum(a, b):
    s = a + b
    t = s - a
    return s, (a - (s - t)) + (b - t)


def quick(a, b):
    s = a + b
    return s, b - (s - a)


def df_add(x, y):
    s, e = two_sum(x[0], y[0])
    return quick(s, e + (x[1] + y[1]))


def df_neg(x):
    return -x[0], -x[1]


def halves(a):
    c = 4097.0 * a
    hi = c - (c - a)
    return hi, a - hi


def two_prod(a, b):
    p = a * b
    ah, al = halves(a)
    bh, bl = halves(b)
    return p, ((ah * bh - p) + ah * bl + al * bh) + al * bl


def df_mul(x, y):
    p, e = two_prod(x[0], y[0])
    return quick(p, e + (x[0] * y[1] + x[1] * y[0]))


def df_div(x, y):
    q = x[0] / y[0]
    p, e = two_prod(q, y[0])
    s, t = two_sum(x[0], -p)
    r = s + (t + (x[1] - (e + q * y[1])))
    return quick(q, r / y[0])


def peers(stage):
    return [o for o in itertools.product(*[range(SIZES[d]) for d in stage]) if any(o)]


def folded(x):
    h = x.shape[0] // 2
    hi, lo = two_sum(x[:h], x[h:])
    while h > 8:
        h //= 2
        s, e = two_sum(hi[:h], hi[h:])
        hi, lo = s, lo[:h] + lo[h:] + e
    return hi, lo


def kernel(
    slot_h, ta_h, ha_h, ev_h, nv_h, ts_h, ss_h, lm_h, od_h,
    out, sol,
    ta, ha, ev, nv, store, lm, od, slot_ref,
    stage, fetched, back, edge, edge_in, rows_out, rows_in, corner_in,
    zed, zed_in, zrow, zrow_in, field, depth, wgt, basis, mail, mail_in,
    load_sem, bulk_sem, halo_sem, zed_sem, mail_sem,
):
    gx, gy = lax.axis_index("gx"), lax.axis_index("gy")
    co = {"xl": gx // 16, "z": (gx // 2) % 8, "c": gx % 2, "xh": gy // 4, "y": gy % 4}

    def peer(st, off):
        n = dict(co)
        for d, o in zip(st, off):
            n[d] = (co[d] + o) % SIZES[d]
        return (n["xl"] * 16 + n["z"] * 2 + n["c"], n["xh"] * 4 + n["y"])

    west, east = (gx + 31) % 32, (gx + 1) % 32
    south, north = (gy + 7) % 8, (gy + 1) % 8
    partner = ((gx + 16) % 32, gy)

    local = [
        (od_h, od), (lm_h.at[0], lm.at[0]), (ha_h, ha),
        (slot_h, slot_ref), (ts_h, store.at[0]), (ss_h, store.at[1]),
        (lm_h.at[pl.ds(1, LEV - 1)], lm.at[pl.ds(1, LEV - 1)]),
        (ta_h, ta), (ev_h, ev), (nv_h, nv),
    ]
    loads = [pltpu.make_async_copy(a, b, load_sem.at[i]) for i, (a, b) in enumerate(local)]
    for c in loads:
        c.start()

    barrier = pltpu.get_barrier_semaphore()
    greeted = [peer(st, off) for st in STAGES for off in peers(st)]
    greeted += [(a, b) for a in (west, east) for b in (south, gy, north)]
    for who in greeted:
        pl.semaphore_signal(barrier, inc=1, device_id=who)

    lane = lax.broadcasted_iota(jnp.int32, (CY, CX), 1)
    row = lax.broadcasted_iota(jnp.int32, (CY, CX), 0)
    lane8 = lane[:8]

    for c in loads[:3]:
        c.wait()
    opened = lm[0].astype(F32)
    target = opened * ha[...]
    dm = opened * od[...]
    field[pl.ds(G, CY), pl.ds(0, CX)] = target
    depth[pl.ds(G, CY), pl.ds(0, CX)] = dm
    edge[...] = jnp.where(
        (lane < 8) | (lane >= 120),
        target,
        jnp.where(lane < 64, pltpu.roll(dm, 8, 1), pltpu.roll(dm, 120, 1)),
    )
    rows_out[0, 0] = target[:8]
    rows_out[0, 1] = dm[:8]
    rows_out[1, 0] = target[120:]
    rows_out[1, 1] = dm[120:]

    for c in loads[3:6]:
        c.wait()
    for k in range(LEV):
        slot = slot_ref[0, 0, k]
        stage[0, k] = store[0, slot]
        stage[1, k] = store[1, slot]

    pl.semaphore_wait(barrier, len(greeted))

    low, high = pl.ds(0, 8), pl.ds(120, 8)
    halo = [
        (edge, edge_in.at[0], (west, gy)),
        (edge, edge_in.at[1], (east, gy)),
        (rows_out.at[0], rows_in.at[0], (gx, south)),
        (rows_out.at[1], rows_in.at[1], (gx, north)),
        (edge.at[low], corner_in.at[0], (west, south)),
        (edge.at[low], corner_in.at[1], (east, south)),
        (edge.at[high], corner_in.at[2], (west, north)),
        (edge.at[high], corner_in.at[3], (east, north)),
    ]
    halos = []
    for i, (a, b, who) in enumerate(halo):
        c = pltpu.make_async_remote_copy(a, b, halo_sem.at[0, i], halo_sem.at[1, i], device_id=who)
        c.start()
        halos.append(c)
    bulks = [
        pltpu.make_async_remote_copy(
            stage.at[:, k], fetched.at[:, k], bulk_sem.at[0, k], bulk_sem.at[1, k], device_id=partner
        )
        for k in range(LEV)
    ]
    for c in bulks[:FIRST]:
        c.start()

    for c in halos:
        c.wait_recv()
    has_north = jnp.where(gy < 7, 1.0, 0.0).astype(F32)
    has_south = jnp.where(gy > 0, 1.0, 0.0).astype(F32)

    def side(east_tile, west_tile, lanes):
        got = jnp.where(lanes < 64, east_tile, west_tile)
        n = got.shape[0]
        inner = jnp.where(lanes < 64, pltpu.roll(got, 120, 1), pltpu.roll(got, 8, 1))
        return got, inner

    mid, top, bottom = pl.ds(G, CY), pl.ds(G + CY, G), pl.ds(0, G)
    own, far = pl.ds(0, CX), pl.ds(CX, CX)
    a, b = side(edge_in[0], edge_in[1], lane)
    field[mid, far] = a
    depth[mid, far] = b
    a, b = side(corner_in[0], corner_in[1], lane8)
    field[top, far] = a * has_north
    depth[top, far] = b * has_north
    a, b = side(corner_in[2], corner_in[3], lane8)
    field[bottom, far] = a * has_south
    depth[bottom, far] = b * has_south
    field[top, own] = rows_in[0, 0] * has_north
    depth[top, own] = rows_in[0, 1] * has_north
    field[bottom, own] = rows_in[1, 0] * has_south
    depth[bottom, own] = rows_in[1, 1] * has_south

    d = depth[...]
    for i, (shift, axis) in enumerate(((COLS - 1, 1), (ROWS - 1, 0))):
        e = pltpu.roll(d, shift, axis)
        wgt[i] = jnp.where((d > 0.0) & (e > 0.0), (STIFFNESS / SPAN * 2.0) * (d + e), 0.0)

    def apply(v):
        fe = wgt[0] * (v - pltpu.roll(v, COLS - 1, 1))
        fn = wgt[1] * (v - pltpu.roll(v, ROWS - 1, 0))
        return (fe - pltpu.roll(fe, 1, 1)) + (fn - pltpu.roll(fn, 1, 0))

    partial = []
    v, before = field[...], None
    for k in range(ITERS):
        image = apply(v)
        if k == 0:
            basis[...] = image
            nxt = 0.5 * image - v
        else:
            nxt = (image - 2.0 * v) - before
        here, there = v[G : G + CY, :CX], nxt[G : G + CY, :CX]
        partial.append(folded(here * here))
        partial.append(folded(here * there))
        v, before = nxt, v
    nm = len(partial)
    hi = jnp.stack([x[0] for x in partial])
    lo = jnp.stack([x[1] for x in partial])
    for s in (4, 2, 1):
        hi, lo = df_add((hi, lo), (pltpu.roll(hi, s, 1), pltpu.roll(lo, s, 1)))
    sub8 = lax.broadcasted_iota(jnp.int32, (8, CX), 0)

    def packed(x):
        done = []
        for first in (0, 8):
            t = jnp.zeros((8, CX), F32)
            for j in range(first, min(first + 8, nm)):
                t = jnp.where(sub8 == j - first, x[j], t)
            done.append(t)
        return jnp.concatenate(done, axis=0)

    hi, lo = packed(hi), packed(lo)
    for s in (64, 32, 16, 8, 4, 2, 1):
        hi, lo = df_add((hi, lo), (pltpu.roll(hi, s, 1), pltpu.roll(lo, s, 1)))
    letter = jnp.where(
        lane8 < 64,
        jnp.where(lane8 < 32, hi[:8], hi[8:]),
        jnp.where(lane8 < 96, lo[:8], lo[8:]),
    )

    def post(st):
        mail[st] = letter
        for i, off in enumerate(peers(STAGES[st])):
            pltpu.make_async_remote_copy(
                mail.at[st], mail_in.at[st, i], mail_sem.at[0, st], mail_sem.at[1, st],
                device_id=peer(STAGES[st], off),
            ).start()

    def collect(st):
        pltpu.make_async_copy(mail_in.at[st], mail_in.at[st], mail_sem.at[1, st]).wait()
        his = [mail[st]] + [mail_in[st, i] for i in range(len(peers(STAGES[st])))]
        terms = [(t, pltpu.roll(t, 64, 1)) for t in his]
        while len(terms) > 1:
            terms = [df_add(terms[i], terms[i + 1]) for i in range(0, len(terms), 2)]
        return terms[0]

    post(0)

    for c in loads[6:]:
        c.wait()
    z = jnp.zeros((CY, CX), F32)
    zn = jnp.zeros((8, CX), F32)
    zs = jnp.zeros((8, CX), F32)
    for k in range(LEV):
        m = lm[k].astype(F32) * ta[k]
        ec = DIFFUSE - 0.5 * ev[k]
        wc = DIFFUSE + 0.5 * ev[k]
        nc = DIFFUSE - 0.5 * nv[k]
        sc = DIFFUSE + 0.5 * nv[k]
        ef, wf, nf, sf = ec * m, wc * m, nc * m, sc * m
        inflow = jnp.where(lane == 0, 0.0, pltpu.roll(ef, 1, 1))
        inflow = inflow + jnp.where(lane == CX - 1, 0.0, pltpu.roll(wf, CX - 1, 1))
        inflow = inflow + jnp.where(row == 0, 0.0, pltpu.roll(nf, 1, 0))
        inflow = inflow + jnp.where(row == CY - 1, 0.0, pltpu.roll(sf, CY - 1, 0))
        back[k] = m + TIMESTEP * (inflow - (ec + wc + nc + sc) * m)
        z = jnp.where(lane == k, pltpu.roll(wf, k, 1) if k else wf, z)
        z = jnp.where(lane == 120 + k, pltpu.roll(ef, 121 + k, 1) if k < 7 else ef, z)
        zrow[1, pl.ds(k, 1)] = nf[CY - 1 :]
        zrow[0, pl.ds(k, 1)] = sf[:1]
    zed[...] = z
    zeds = []
    for i, (a, b, who) in enumerate((
        (zed, zed_in.at[0], (west, gy)),
        (zed, zed_in.at[1], (east, gy)),
        (zrow.at[0], zrow_in.at[0], (gx, south)),
        (zrow.at[1], zrow_in.at[1], (gx, north)),
    )):
        c = pltpu.make_async_remote_copy(a, b, zed_sem.at[0, i], zed_sem.at[1, i], device_id=who)
        c.start()
        zeds.append(c)

    total = collect(0)
    letter = jnp.where(lane8 < 64, total[0], pltpu.roll(total[1], 64, 1))
    post(1)

    for c in bulks[FIRST:]:
        c.start()

    total = collect(1)
    cur = tuple(jnp.concatenate([t, pltpu.roll(t, 96, 1)], axis=0) for t in total)
    order = lax.broadcasted_iota(jnp.int32, cur[0].shape, 0)
    later = order >= 2
    base = [jnp.where(later, jnp.where(order % 2 == 0, x[:1], x[1:2]), 0.0) for x in cur]
    cur = df_add([jnp.where(later, 2.0 * x, x) for x in cur], [-x for x in base])
    shrink = jnp.ones(cur[0].shape, F32)
    for k in range(2, 2 * ITERS):
        shrink = jnp.where(order >= k, 0.5 * shrink, shrink)
    cur = (cur[0] * shrink, cur[1] * shrink)
    couple = jnp.where(order == 1, 0.5, 0.25)
    prev = None

    def pick(x, k):
        return x[0][k : k + 1], x[1][k : k + 1]

    def spread(x):
        return jnp.broadcast_to(x[0], cur[0].shape), jnp.broadcast_to(x[1], cur[0].shape)

    def up(x):
        return pltpu.roll(x[0], 15, 0), pltpu.roll(x[1], 15, 0)

    def down(x):
        return couple * pltpu.roll(x[0], 1, 0), couple * pltpu.roll(x[1], 1, 0)

    norm = pick(cur, 0)
    ratio = df_div(pick(cur, 1), norm)
    ja, jb = [ratio], []
    for k in range(1, ITERS):
        nxt = df_add(df_add(up(cur), down(cur)), df_neg(df_mul(spread(ja[-1]), cur)))
        if k > 1:
            nxt = df_add(nxt, df_neg(df_mul(spread(jb[-1]), prev)))
        fresh = pick(nxt, k)
        new_ratio = df_div(pick(nxt, k + 1), fresh)
        ja.append(df_add(new_ratio, df_neg(ratio)))
        jb.append(df_div(fresh, norm))
        norm, ratio, prev, cur = fresh, new_ratio, cur, nxt
    steps, growths = [], []
    for k in range(ITERS):
        diag = 1.0 + (SPAN / 2.0) * ((1.0 + ja[k][0]) + ja[k][1])
        if k:
            off = (SPAN * SPAN / 4.0) * (jb[k - 1][0] + jb[k - 1][1])
            growths.append(off * steps[-1] * steps[-1])
            diag = diag - off * steps[-1]
        steps.append(1.0 / diag)
    whole = (ROWS, COLS)
    steps = [jnp.broadcast_to(x[:1, :1], whole) for x in steps]
    growths = [jnp.broadcast_to(x[:1, :1], whole) for x in growths]

    r = field[...]
    p = r
    s = jnp.zeros_like(r)
    for k in range(ITERS):
        s = s + steps[k] * p
        if k + 1 < ITERS:
            q = p + (SPAN / 4.0) * (basis[...] if k == 0 else apply(p))
            r = r - steps[k] * q
            p = r + growths[k] * p
    load = depth[...] * s
    flow_e = jnp.where(wgt[0] > 0.0, pltpu.roll(load, COLS - 1, 1) - load, 0.0)
    flow_n = jnp.where(wgt[1] > 0.0, pltpu.roll(load, ROWS - 1, 0) - load, 0.0)
    pull = (flow_e - pltpu.roll(flow_e, 1, 1)) + (flow_n - pltpu.roll(flow_n, 1, 0))
    sol[...] = s[G : G + CY, :CX]
    pressure = -GRAVITY * pull[G : G + CY, :CX]
    for c in zeds:
        c.wait_recv()
    ze, zw = zed_in[0], zed_in[1]
    for k in range(LEV):
        b = back[k]
        b = b + jnp.where(lane == 0, pltpu.roll(zw, 8 - k, 1), 0.0)
        b = b + jnp.where(lane == CX - 1, pltpu.roll(ze, 127 - k, 1), 0.0)
        b = b + jnp.where(row == 0, zrow_in[1, pl.ds(k, 1)] * has_south, 0.0)
        b = b + jnp.where(row == CY - 1, zrow_in[0, pl.ds(k, 1)] * has_north, 0.0)
        dens = ((1.0 + k / LEV) * pressure) * lm[k].astype(F32)
        bulks[k].wait_recv()
        ct, cs = fetched[0, k], fetched[1, k]
        out[0, k] = b + (THERMAL + 2.0 * NONLINEAR * ct + CABBELING * cs) * dens
        out[1, k] = (HALINE + CABBELING * ct) * dens
    for c in halos + bulks + zeds:
        c.wait_send()
    for st in range(2):
        pltpu.make_async_copy(mail_in.at[st], mail_in.at[st], mail_sem.at[0, st]).wait()


def deliver(both, sol, tb_h, sb_h, sa_h, sem):
    copies = [
        pltpu.make_async_copy(a, b, sem.at[i])
        for i, (a, b) in enumerate(((both.at[0], tb_h), (both.at[1], sb_h), (sol, sa_h)))
    ]
    for c in copies:
        c.start()
    for c in copies:
        c.wait()


def body(ta, ha, ev, nv, ts, ss, slots, lm, od):
    vm = lambda *shape: pltpu.VMEM(shape, F32)
    cube = (LEV, CY, CX)
    dma = lambda *shape: pltpu.SemaphoreType.DMA(shape)
    n = len(peers(STAGES[0]))
    hbm = pl.BlockSpec(memory_space=pltpu.HBM)
    vmem = pl.BlockSpec(memory_space=pltpu.VMEM)
    both, sol = pl.pallas_call(
        kernel,
        out_shape=(jax.ShapeDtypeStruct((2,) + cube, F32), jax.ShapeDtypeStruct((CY, CX), F32)),
        in_specs=[hbm] * 9,
        out_specs=(vmem, vmem),
        scratch_shapes=[
            vm(*cube), vm(CY, CX), vm(*cube), vm(*cube), vm(2, *cube), pltpu.VMEM(cube, jnp.int32), vm(CY, CX),
            pltpu.SMEM((1, 1, LEV), jnp.int32),
            vm(2, *cube), vm(2, *cube), vm(*cube),
            vm(CY, CX), vm(2, CY, CX), vm(2, 2, 8, CX), vm(2, 2, 8, CX), vm(4, 8, CX),
            vm(CY, CX), vm(2, CY, CX), vm(2, 8, CX), vm(2, 8, CX),
            vm(ROWS, COLS), vm(ROWS, COLS), vm(2, ROWS, COLS), vm(ROWS, COLS),
            vm(2, 8, CX), vm(2, n, 8, CX),
            dma(10), dma(2, LEV), dma(2, 8), dma(2, 4), dma(2, 2),
        ],
        compiler_params=pltpu.CompilerParams(
            collective_id=0, has_side_effects=True, vmem_limit_bytes=40 << 20
        ),
        cost_estimate=pl.CostEstimate(flops=40000000, bytes_accessed=60000000, transcendentals=0),
        name="adjoint",
    )(*[pltpu.with_memory_space_constraint(x, pltpu.HBM) for x in (slots, ta, ha, ev, nv, ts, ss, lm, od)])
    return pl.pallas_call(
        deliver,
        out_shape=(
            jax.ShapeDtypeStruct(cube, F32),
            jax.ShapeDtypeStruct(cube, F32),
            jax.ShapeDtypeStruct((CY, CX), F32),
        ),
        in_specs=[vmem, vmem],
        out_specs=(hbm, hbm, hbm),
        scratch_shapes=[dma(3)],
        name="deliver",
    )(*[pltpu.with_memory_space_constraint(x, pltpu.VMEM) for x in (both, sol)])


def solution(mesh):
    cube, flat = P(None, "gy", "gx"), P("gy", "gx")
    return jax.shard_map(
        body,
        mesh=mesh,
        in_specs=(cube, flat, cube, cube, cube, cube, P("gx", "gy", None), cube, flat),
        out_specs=(cube, cube, flat),
        check_vma=False,
    )
```

```python
import itertools
import functools

import jax
import jax.numpy as jnp
from jax import lax
from jax.experimental import pallas as pl
from jax.experimental.pallas import tpu as pltpu
from jax.sharding import PartitionSpec as P

DIFFUSE = 0.2
TIMESTEP = 1.0
STIFFNESS = 8.0
GRAVITY = 4.0
THERMAL = 0.5
NONLINEAR = 0.4
CABBELING = 0.3
HALINE = 0.8
ITERS = 6
SPAN = 8.0
G = 8
BATCH = (4, 0, 0, 0, 1)
LEV, CY, CX = 8, 128, 128
ROWS, COLS = CY + 2 * G, 2 * CX
SIZES = {"xl": 2, "z": 8, "c": 2, "xh": 2, "y": 4}
STAGES = (("z", "c"), ("xl", "xh", "y"))
HOPS = {"xl": 1.0, "z": 1.0, "c": 0.3, "xh": 2.0, "y": 1.0}
F32 = jnp.float32


def two_sum(a, b):
    s = a + b
    t = s - a
    return s, (a - (s - t)) + (b - t)


def quick(a, b):
    s = a + b
    return s, b - (s - a)


def df_add(x, y):
    s, e = two_sum(x[0], y[0])
    return quick(s, e + (x[1] + y[1]))


def df_neg(x):
    return -x[0], -x[1]


def halves(a):
    c = 4097.0 * a
    hi = c - (c - a)
    return hi, a - hi


def two_prod(a, b):
    p = a * b
    ah, al = halves(a)
    bh, bl = halves(b)
    return p, ((ah * bh - p) + ah * bl + al * bh) + al * bl


def df_mul(x, y):
    p, e = two_prod(x[0], y[0])
    return quick(p, e + (x[0] * y[1] + x[1] * y[0]))


def df_div(x, y):
    q = x[0] / y[0]
    p, e = two_prod(q, y[0])
    s, t = two_sum(x[0], -p)
    r = s + (t + (x[1] - (e + q * y[1])))
    return quick(q, r / y[0])


def peers(stage):
    offs = [o for o in itertools.product(*[range(SIZES[d]) for d in stage]) if any(o)]
    return sorted(offs, key=lambda o: -sum(HOPS[d] * min(k, SIZES[d] - k) for d, k in zip(stage, o)))


def folded(x):
    h = x.shape[0] // 2
    hi, lo = two_sum(x[:h], x[h:])
    while h > 8:
        h //= 2
        s, e = two_sum(hi[:h], hi[h:])
        hi, lo = s, lo[:h] + lo[h:] + e
    return hi, lo


def kernel(
    slot_h, ta_h, ha_h, ev_h, nv_h, ts_h, ss_h, lm_h, od_h,
    out, sol,
    ta, ha, ev, nv, store, lm, od, slot_ref,
    stage, fetched, back, edge, edge_in, rows_out, rows_in, corner_in,
    zed, zed_in, zrow, zrow_in, field, depth, wgt, basis, mail, mail_in,
    load_sem, bulk_sem, halo_sem, zed_sem, mail_sem, ready_sem,
):
    gx, gy = lax.axis_index("gx"), lax.axis_index("gy")
    co = {"xl": gx // 16, "z": (gx // 2) % 8, "c": gx % 2, "xh": gy // 4, "y": gy % 4}

    def peer(st, off):
        n = dict(co)
        for d, o in zip(st, off):
            n[d] = (co[d] + o) % SIZES[d]
        return (n["xl"] * 16 + n["z"] * 2 + n["c"], n["xh"] * 4 + n["y"])

    west, east = (gx + 31) % 32, (gx + 1) % 32
    south, north = (gy + 7) % 8, (gy + 1) % 8
    partner = ((gx + 16) % 32, gy)

    local = [
        (od_h, od), (lm_h.at[0], lm.at[0]), (ha_h, ha),
        (slot_h, slot_ref), (ts_h, store.at[0]), (ss_h, store.at[1]),
        (lm_h.at[pl.ds(1, LEV - 1)], lm.at[pl.ds(1, LEV - 1)]),
        (ta_h, ta), (ev_h, ev), (nv_h, nv),
    ]
    loads = [pltpu.make_async_copy(a, b, load_sem.at[i]) for i, (a, b) in enumerate(local)]
    for c in loads:
        c.start()

    barrier = pltpu.get_barrier_semaphore()
    greeted = [peer(STAGES[1], off) for off in peers(STAGES[1])]
    greeted += [peer(STAGES[0], off) for off in ((1, 0), (1, 1), (7, 0), (7, 1))]
    greeted += [(a, b) for a in (west, east) for b in (south, gy, north)]
    for who in greeted:
        pl.semaphore_signal(barrier, inc=1, device_id=who)

    lane = lax.broadcasted_iota(jnp.int32, (CY, CX), 1)
    row = lax.broadcasted_iota(jnp.int32, (CY, CX), 0)
    lane8 = lane[:8]

    for c in loads[:3]:
        c.wait()
    opened = lm[0].astype(F32)
    target = opened * ha[...]
    dm = opened * od[...]
    field[pl.ds(G, CY), pl.ds(0, CX)] = target
    depth[pl.ds(G, CY), pl.ds(0, CX)] = dm
    edge[...] = jnp.where(
        (lane < 8) | (lane >= 120),
        target,
        jnp.where(lane < 64, pltpu.roll(dm, 8, 1), pltpu.roll(dm, 120, 1)),
    )
    rows_out[0, 0] = target[:8]
    rows_out[0, 1] = dm[:8]
    rows_out[1, 0] = target[120:]
    rows_out[1, 1] = dm[120:]

    for c in loads[3:6]:
        c.wait()
    for k in range(LEV):
        slot = slot_ref[0, 0, k]
        stage[0, k] = store[0, slot]
        stage[1, k] = store[1, slot]

    pl.semaphore_wait(barrier, len(greeted))

    low, high = pl.ds(0, 8), pl.ds(120, 8)
    halo = [
        (edge, edge_in.at[0], (west, gy)),
        (edge, edge_in.at[1], (east, gy)),
        (rows_out.at[0], rows_in.at[0], (gx, south)),
        (rows_out.at[1], rows_in.at[1], (gx, north)),
        (edge.at[low], corner_in.at[0], (west, south)),
        (edge.at[low], corner_in.at[1], (east, south)),
        (edge.at[high], corner_in.at[2], (west, north)),
        (edge.at[high], corner_in.at[3], (east, north)),
    ]
    halos = []
    for i, (a, b, who) in enumerate(halo):
        c = pltpu.make_async_remote_copy(a, b, halo_sem.at[0, i], halo_sem.at[1, i], device_id=who)
        c.start()
        halos.append(c)
    bulks = [
        pltpu.make_async_remote_copy(
            stage.at[:, k], fetched.at[:, k], bulk_sem.at[0, k], bulk_sem.at[1, k], device_id=partner
        )
        for k in range(LEV)
    ]
    def ready(step):
        for i, off in enumerate((step, 8 - step)):
            pl.semaphore_signal(ready_sem.at[step - 1, i], inc=1, device_id=peer(("z",), (off,)))

    def await_ready(step):
        for i in range(2):
            pl.semaphore_wait(ready_sem.at[step - 1, i], 1)

    ready(1)
    queue = list(bulks)

    def feed(count):
        for c in queue[:count]:
            c.start()
        del queue[:count]

    feed(BATCH[0])
    for group, count in zip((halos[:2], halos[2:4], halos[4:]), BATCH[1:4]):
        for c in group:
            c.wait_recv()
        feed(count)
        if group[0] is halos[0]:
            await_ready(1)
            ready(2)
    has_north = jnp.where(gy < 7, 1.0, 0.0).astype(F32)
    has_south = jnp.where(gy > 0, 1.0, 0.0).astype(F32)

    def side(east_tile, west_tile, lanes):
        got = jnp.where(lanes < 64, east_tile, west_tile)
        n = got.shape[0]
        inner = jnp.where(lanes < 64, pltpu.roll(got, 120, 1), pltpu.roll(got, 8, 1))
        return got, inner

    mid, top, bottom = pl.ds(G, CY), pl.ds(G + CY, G), pl.ds(0, G)
    own, far = pl.ds(0, CX), pl.ds(CX, CX)
    a, b = side(edge_in[0], edge_in[1], lane)
    field[mid, far] = a
    depth[mid, far] = b
    a, b = side(corner_in[0], corner_in[1], lane8)
    field[top, far] = a * has_north
    depth[top, far] = b * has_north
    a, b = side(corner_in[2], corner_in[3], lane8)
    field[bottom, far] = a * has_south
    depth[bottom, far] = b * has_south
    field[top, own] = rows_in[0, 0] * has_north
    depth[top, own] = rows_in[0, 1] * has_north
    field[bottom, own] = rows_in[1, 0] * has_south
    depth[bottom, own] = rows_in[1, 1] * has_south

    d = depth[...]
    for i, (shift, axis) in enumerate(((COLS - 1, 1), (ROWS - 1, 0))):
        e = pltpu.roll(d, shift, axis)
        wgt[i] = jnp.where((d > 0.0) & (e > 0.0), (STIFFNESS / SPAN * 2.0) * (d + e), 0.0)

    def apply(v):
        fe = wgt[0] * (v - pltpu.roll(v, COLS - 1, 1))
        fn = wgt[1] * (v - pltpu.roll(v, ROWS - 1, 0))
        return (fe - pltpu.roll(fe, 1, 1)) + (fn - pltpu.roll(fn, 1, 0))

    partial = []
    v, before = field[...], None
    for k in range(ITERS):
        image = apply(v)
        if k == 0:
            basis[...] = image
            nxt = 0.5 * image - v
        else:
            nxt = (image - 2.0 * v) - before
        here, there = v[G : G + CY, :CX], nxt[G : G + CY, :CX]
        partial.append(folded(here * here))
        partial.append(folded(here * there))
        v, before = nxt, v
    nm = len(partial)
    hi = jnp.stack([x[0] for x in partial])
    lo = jnp.stack([x[1] for x in partial])
    for s in (4, 2, 1):
        hi, lo = df_add((hi, lo), (pltpu.roll(hi, s, 1), pltpu.roll(lo, s, 1)))
    sub8 = lax.broadcasted_iota(jnp.int32, (8, CX), 0)

    def packed(x):
        done = []
        for first in (0, 8):
            t = jnp.zeros((8, CX), F32)
            for j in range(first, min(first + 8, nm)):
                t = jnp.where(sub8 == j - first, x[j], t)
            done.append(t)
        return jnp.concatenate(done, axis=0)

    hi, lo = packed(hi), packed(lo)
    for s in (64, 32, 16, 8, 4, 2, 1):
        hi, lo = df_add((hi, lo), (pltpu.roll(hi, s, 1), pltpu.roll(lo, s, 1)))
    letter = jnp.where(
        lane8 < 64,
        jnp.where(lane8 < 32, hi[:8], hi[8:]),
        jnp.where(lane8 < 96, lo[:8], lo[8:]),
    )

    def post(st):
        mail[st] = letter
        for i, off in enumerate(peers(STAGES[st])):
            pltpu.make_async_remote_copy(
                mail.at[st], mail_in.at[st, i], mail_sem.at[0, st], mail_sem.at[1, st],
                device_id=peer(STAGES[st], off),
            ).start()

    def collect(st):
        pltpu.make_async_copy(mail_in.at[st], mail_in.at[st], mail_sem.at[1, st]).wait()
        his = [mail[st]] + [mail_in[st, i] for i in range(len(peers(STAGES[st])))]
        terms = [(t, pltpu.roll(t, 64, 1)) for t in his]
        while len(terms) > 1:
            terms = [df_add(terms[i], terms[i + 1]) for i in range(0, len(terms), 2)]
        return terms[0]

    await_ready(2)
    post(0)
    feed(BATCH[4])

    for c in loads[6:]:
        c.wait()
    z = jnp.zeros((CY, CX), F32)
    zn = jnp.zeros((8, CX), F32)
    zs = jnp.zeros((8, CX), F32)
    for k in range(LEV):
        m = lm[k].astype(F32) * ta[k]
        ec = DIFFUSE - 0.5 * ev[k]
        wc = DIFFUSE + 0.5 * ev[k]
        nc = DIFFUSE - 0.5 * nv[k]
        sc = DIFFUSE + 0.5 * nv[k]
        ef, wf, nf, sf = ec * m, wc * m, nc * m, sc * m
        inflow = jnp.where(lane == 0, 0.0, pltpu.roll(ef, 1, 1))
        inflow = inflow + jnp.where(lane == CX - 1, 0.0, pltpu.roll(wf, CX - 1, 1))
        inflow = inflow + jnp.where(row == 0, 0.0, pltpu.roll(nf, 1, 0))
        inflow = inflow + jnp.where(row == CY - 1, 0.0, pltpu.roll(sf, CY - 1, 0))
        back[k] = m + TIMESTEP * (inflow - (ec + wc + nc + sc) * m)
        z = jnp.where(lane == k, pltpu.roll(wf, k, 1) if k else wf, z)
        z = jnp.where(lane == 120 + k, pltpu.roll(ef, 121 + k, 1) if k < 7 else ef, z)
        zrow[1, pl.ds(k, 1)] = nf[CY - 1 :]
        zrow[0, pl.ds(k, 1)] = sf[:1]
    zed[...] = z
    zeds = []
    for i, (a, b, who) in enumerate((
        (zed, zed_in.at[0], (west, gy)),
        (zed, zed_in.at[1], (east, gy)),
        (zrow.at[0], zrow_in.at[0], (gx, south)),
        (zrow.at[1], zrow_in.at[1], (gx, north)),
    )):
        c = pltpu.make_async_remote_copy(a, b, zed_sem.at[0, i], zed_sem.at[1, i], device_id=who)
        c.start()
        zeds.append(c)

    total = collect(0)
    letter = jnp.where(lane8 < 64, total[0], pltpu.roll(total[1], 64, 1))
    post(1)
    feed(LEV)

    total = collect(1)
    cur = tuple(jnp.concatenate([t, pltpu.roll(t, 96, 1)], axis=0) for t in total)
    order = lax.broadcasted_iota(jnp.int32, cur[0].shape, 0)
    later = order >= 2
    base = [jnp.where(later, jnp.where(order % 2 == 0, x[:1], x[1:2]), 0.0) for x in cur]
    cur = df_add([jnp.where(later, 2.0 * x, x) for x in cur], [-x for x in base])
    shrink = jnp.ones(cur[0].shape, F32)
    for k in range(2, 2 * ITERS):
        shrink = jnp.where(order >= k, 0.5 * shrink, shrink)
    cur = (cur[0] * shrink, cur[1] * shrink)
    couple = jnp.where(order == 1, 0.5, 0.25)
    prev = None

    def pick(x, k):
        return x[0][k : k + 1], x[1][k : k + 1]

    def spread(x):
        return jnp.broadcast_to(x[0], cur[0].shape), jnp.broadcast_to(x[1], cur[0].shape)

    def up(x):
        return pltpu.roll(x[0], 15, 0), pltpu.roll(x[1], 15, 0)

    def down(x):
        return couple * pltpu.roll(x[0], 1, 0), couple * pltpu.roll(x[1], 1, 0)

    norm = pick(cur, 0)
    ratio = df_div(pick(cur, 1), norm)
    ja, jb = [ratio], []
    for k in range(1, ITERS):
        nxt = df_add(df_add(up(cur), down(cur)), df_neg(df_mul(spread(ja[-1]), cur)))
        if k > 1:
            nxt = df_add(nxt, df_neg(df_mul(spread(jb[-1]), prev)))
        fresh = pick(nxt, k)
        new_ratio = df_div(pick(nxt, k + 1), fresh)
        ja.append(df_add(new_ratio, df_neg(ratio)))
        jb.append(df_div(fresh, norm))
        norm, ratio, prev, cur = fresh, new_ratio, cur, nxt
    steps, growths = [], []
    for k in range(ITERS):
        diag = 1.0 + (SPAN / 2.0) * ((1.0 + ja[k][0]) + ja[k][1])
        if k:
            off = (SPAN * SPAN / 4.0) * (jb[k - 1][0] + jb[k - 1][1])
            growths.append(off * steps[-1] * steps[-1])
            diag = diag - off * steps[-1]
        steps.append(1.0 / diag)
    whole = (ROWS, COLS)
    steps = [jnp.broadcast_to(x[:1, :1], whole) for x in steps]
    growths = [jnp.broadcast_to(x[:1, :1], whole) for x in growths]

    r = field[...]
    p = r
    s = jnp.zeros_like(r)
    for k in range(ITERS):
        s = s + steps[k] * p
        if k + 1 < ITERS:
            q = p + (SPAN / 4.0) * (basis[...] if k == 0 else apply(p))
            r = r - steps[k] * q
            p = r + growths[k] * p
    load = depth[...] * s
    flow_e = jnp.where(wgt[0] > 0.0, pltpu.roll(load, COLS - 1, 1) - load, 0.0)
    flow_n = jnp.where(wgt[1] > 0.0, pltpu.roll(load, ROWS - 1, 0) - load, 0.0)
    pull = (flow_e - pltpu.roll(flow_e, 1, 1)) + (flow_n - pltpu.roll(flow_n, 1, 0))
    sol[...] = s[G : G + CY, :CX]
    pressure = -GRAVITY * pull[G : G + CY, :CX]
    for c in zeds:
        c.wait_recv()
    ze, zw = zed_in[0], zed_in[1]
    for k in range(LEV):
        b = back[k]
        b = b + jnp.where(lane == 0, pltpu.roll(zw, 8 - k, 1), 0.0)
        b = b + jnp.where(lane == CX - 1, pltpu.roll(ze, 127 - k, 1), 0.0)
        b = b + jnp.where(row == 0, zrow_in[1, pl.ds(k, 1)] * has_south, 0.0)
        b = b + jnp.where(row == CY - 1, zrow_in[0, pl.ds(k, 1)] * has_north, 0.0)
        dens = ((1.0 + k / LEV) * pressure) * lm[k].astype(F32)
        bulks[k].wait_recv()
        ct, cs = fetched[0, k], fetched[1, k]
        out[0, k] = b + (THERMAL + 2.0 * NONLINEAR * ct + CABBELING * cs) * dens
        out[1, k] = (HALINE + CABBELING * ct) * dens
    for c in halos + bulks + zeds:
        c.wait_send()
    for st in range(2):
        pltpu.make_async_copy(mail_in.at[st], mail_in.at[st], mail_sem.at[0, st]).wait()


def deliver(both, sol, tb_h, sb_h, sa_h, sem):
    copies = [
        pltpu.make_async_copy(a, b, sem.at[i])
        for i, (a, b) in enumerate(((both.at[0], tb_h), (both.at[1], sb_h), (sol, sa_h)))
    ]
    for c in copies:
        c.start()
    for c in copies:
        c.wait()


def body(ta, ha, ev, nv, ts, ss, slots, lm, od):
    vm = lambda *shape: pltpu.VMEM(shape, F32)
    cube = (LEV, CY, CX)
    dma = lambda *shape: pltpu.SemaphoreType.DMA(shape)
    n = len(peers(STAGES[0]))
    hbm = pl.BlockSpec(memory_space=pltpu.HBM)
    vmem = pl.BlockSpec(memory_space=pltpu.VMEM)
    both, sol = pl.pallas_call(
        kernel,
        out_shape=(jax.ShapeDtypeStruct((2,) + cube, F32), jax.ShapeDtypeStruct((CY, CX), F32)),
        in_specs=[hbm] * 9,
        out_specs=(vmem, vmem),
        scratch_shapes=[
            vm(*cube), vm(CY, CX), vm(*cube), vm(*cube), vm(2, *cube), pltpu.VMEM(cube, jnp.int32), vm(CY, CX),
            pltpu.SMEM((1, 1, LEV), jnp.int32),
            vm(2, *cube), vm(2, *cube), vm(*cube),
            vm(CY, CX), vm(2, CY, CX), vm(2, 2, 8, CX), vm(2, 2, 8, CX), vm(4, 8, CX),
            vm(CY, CX), vm(2, CY, CX), vm(2, 8, CX), vm(2, 8, CX),
            vm(ROWS, COLS), vm(ROWS, COLS), vm(2, ROWS, COLS), vm(ROWS, COLS),
            vm(2, 8, CX), vm(2, n, 8, CX),
            dma(10), dma(2, LEV), dma(2, 8), dma(2, 4), dma(2, 2), pltpu.SemaphoreType.REGULAR((2, 2)),
        ],
        compiler_params=pltpu.CompilerParams(
            collective_id=0, has_side_effects=True, vmem_limit_bytes=40 << 20
        ),
        cost_estimate=pl.CostEstimate(flops=40000000, bytes_accessed=60000000, transcendentals=0),
        name="adjoint",
    )(*[pltpu.with_memory_space_constraint(x, pltpu.HBM) for x in (slots, ta, ha, ev, nv, ts, ss, lm, od)])
    return pl.pallas_call(
        deliver,
        out_shape=(
            jax.ShapeDtypeStruct(cube, F32),
            jax.ShapeDtypeStruct(cube, F32),
            jax.ShapeDtypeStruct((CY, CX), F32),
        ),
        in_specs=[vmem, vmem],
        out_specs=(hbm, hbm, hbm),
        scratch_shapes=[dma(3)],
        name="deliver",
    )(*[pltpu.with_memory_space_constraint(x, pltpu.VMEM) for x in (both, sol)])


def solution(mesh):
    cube, flat = P(None, "gy", "gx"), P("gy", "gx")
    return jax.shard_map(
        body,
        mesh=mesh,
        in_specs=(cube, flat, cube, cube, cube, cube, P("gx", "gy", None), cube, flat),
        out_specs=(cube, cube, flat),
        check_vma=False,
    )
```

```python
import itertools
import functools

import jax
import jax.numpy as jnp
from jax import lax
from jax.experimental import pallas as pl
from jax.experimental.pallas import tpu as pltpu
from jax.sharding import PartitionSpec as P

DIFFUSE = 0.2
TIMESTEP = 1.0
STIFFNESS = 8.0
GRAVITY = 4.0
THERMAL = 0.5
NONLINEAR = 0.4
CABBELING = 0.3
HALINE = 0.8
ITERS = 6
SPAN = 8.0
G = 8
BATCH = (5, 0, 0, 0, 0)
LEV, CY, CX = 8, 128, 128
ROWS, COLS = CY + 2 * G, 2 * CX
SIZES = {"xl": 2, "z": 8, "c": 2, "xh": 2, "y": 4}
STAGES = (("z", "c"), ("xl", "xh", "y"))
HOPS = {"xl": 1.0, "z": 1.0, "c": 0.3, "xh": 2.0, "y": 1.0}
F32 = jnp.float32


def two_sum(a, b):
    s = a + b
    t = s - a
    return s, (a - (s - t)) + (b - t)


def quick(a, b):
    s = a + b
    return s, b - (s - a)


def df_add(x, y):
    s, e = two_sum(x[0], y[0])
    return quick(s, e + (x[1] + y[1]))


def df_neg(x):
    return -x[0], -x[1]


def halves(a):
    c = 4097.0 * a
    hi = c - (c - a)
    return hi, a - hi


def two_prod(a, b):
    p = a * b
    ah, al = halves(a)
    bh, bl = halves(b)
    return p, ((ah * bh - p) + ah * bl + al * bh) + al * bl


def df_mul(x, y):
    p, e = two_prod(x[0], y[0])
    return quick(p, e + (x[0] * y[1] + x[1] * y[0]))


def df_div(x, y):
    q = x[0] / y[0]
    p, e = two_prod(q, y[0])
    s, t = two_sum(x[0], -p)
    r = s + (t + (x[1] - (e + q * y[1])))
    return quick(q, r / y[0])


def peers(stage):
    offs = [o for o in itertools.product(*[range(SIZES[d]) for d in stage]) if any(o)]
    return sorted(offs, key=lambda o: -sum(HOPS[d] * min(k, SIZES[d] - k) for d, k in zip(stage, o)))


def folded(x):
    h = x.shape[0] // 2
    hi, lo = two_sum(x[:h], x[h:])
    while h > 8:
        h //= 2
        s, e = two_sum(hi[:h], hi[h:])
        hi, lo = s, lo[:h] + lo[h:] + e
    return hi, lo


def kernel(
    slot_h, ta_h, ha_h, ev_h, nv_h, ts_h, ss_h, lm_h, od_h,
    out, sol,
    ta, ha, ev, nv, store, lm, od, slot_ref,
    stage, fetched, back, edge, edge_in, rows_out, rows_in, corner_in,
    zed, zed_in, zrow, zrow_in, field, depth, wgt, basis, mail, mail_in,
    load_sem, bulk_sem, halo_sem, zed_sem, mail_sem, ready_sem,
):
    gx, gy = lax.axis_index("gx"), lax.axis_index("gy")
    co = {"xl": gx // 16, "z": (gx // 2) % 8, "c": gx % 2, "xh": gy // 4, "y": gy % 4}

    def peer(st, off):
        n = dict(co)
        for d, o in zip(st, off):
            n[d] = (co[d] + o) % SIZES[d]
        return (n["xl"] * 16 + n["z"] * 2 + n["c"], n["xh"] * 4 + n["y"])

    west, east = (gx + 31) % 32, (gx + 1) % 32
    south, north = (gy + 7) % 8, (gy + 1) % 8
    partner = ((gx + 16) % 32, gy)

    barrier = pltpu.get_barrier_semaphore()
    greeted = [(a, b) for a in (west, east) for b in (south, north, gy)]
    greeted += [peer(STAGES[1], off) for off in peers(STAGES[1])]
    greeted += [peer(STAGES[0], off) for off in ((1, 0), (1, 1), (7, 0), (7, 1))]
    for who in greeted:
        pl.semaphore_signal(barrier, inc=1, device_id=who)

    local = [
        (od_h, od), (lm_h.at[0], lm.at[0]), (ha_h, ha),
        (slot_h, slot_ref), (ts_h, store.at[0]), (ss_h, store.at[1]),
        (lm_h.at[pl.ds(1, LEV - 1)], lm.at[pl.ds(1, LEV - 1)]),
        (ta_h, ta), (ev_h, ev), (nv_h, nv),
    ]
    loads = [pltpu.make_async_copy(a, b, load_sem.at[i]) for i, (a, b) in enumerate(local)]
    for c in loads:
        c.start()

    lane = lax.broadcasted_iota(jnp.int32, (CY, CX), 1)
    row = lax.broadcasted_iota(jnp.int32, (CY, CX), 0)
    lane8 = lane[:8]

    for c in loads[:3]:
        c.wait()
    opened = lm[0].astype(F32)
    target = opened * ha[...]
    dm = opened * od[...]
    field[pl.ds(G, CY), pl.ds(0, CX)] = target
    depth[pl.ds(G, CY), pl.ds(0, CX)] = dm
    edge[...] = jnp.where(
        (lane < 8) | (lane >= 120),
        target,
        jnp.where(lane < 64, pltpu.roll(dm, 8, 1), pltpu.roll(dm, 120, 1)),
    )
    rows_out[0, 0] = target[:8]
    rows_out[0, 1] = dm[:8]
    rows_out[1, 0] = target[120:]
    rows_out[1, 1] = dm[120:]

    for c in loads[3:6]:
        c.wait()
    for k in range(LEV):
        slot = slot_ref[0, 0, k]
        stage[0, k] = store[0, slot]
        stage[1, k] = store[1, slot]

    pl.semaphore_wait(barrier, len(greeted))

    low, high = pl.ds(0, 8), pl.ds(120, 8)
    halo = [
        (edge, edge_in.at[0], (west, gy)),
        (edge, edge_in.at[1], (east, gy)),
        (rows_out.at[0], rows_in.at[0], (gx, south)),
        (rows_out.at[1], rows_in.at[1], (gx, north)),
        (edge.at[low], corner_in.at[0], (west, south)),
        (edge.at[low], corner_in.at[1], (east, south)),
        (edge.at[high], corner_in.at[2], (west, north)),
        (edge.at[high], corner_in.at[3], (east, north)),
    ]
    halos = []
    for i, (a, b, who) in enumerate(halo):
        c = pltpu.make_async_remote_copy(a, b, halo_sem.at[0, i], halo_sem.at[1, i], device_id=who)
        c.start()
        halos.append(c)
    bulks = [
        pltpu.make_async_remote_copy(
            stage.at[:, k], fetched.at[:, k], bulk_sem.at[0, k], bulk_sem.at[1, k], device_id=partner
        )
        for k in range(LEV)
    ]
    def ready(step):
        for i, off in enumerate((step, 8 - step)):
            pl.semaphore_signal(ready_sem.at[step - 1, i], inc=1, device_id=peer(("z",), (off,)))

    def await_ready(step):
        for i in range(2):
            pl.semaphore_wait(ready_sem.at[step - 1, i], 1)

    ready(1)
    queue = list(bulks)

    def feed(count):
        for c in queue[:count]:
            c.start()
        del queue[:count]

    feed(BATCH[0])
    for group, count in zip((halos[:2], halos[2:4], halos[4:]), BATCH[1:4]):
        for c in group:
            c.wait_recv()
        feed(count)
        if group[0] is halos[0]:
            await_ready(1)
            ready(2)
    has_north = jnp.where(gy < 7, 1.0, 0.0).astype(F32)
    has_south = jnp.where(gy > 0, 1.0, 0.0).astype(F32)

    def side(east_tile, west_tile, lanes):
        got = jnp.where(lanes < 64, east_tile, west_tile)
        n = got.shape[0]
        inner = jnp.where(lanes < 64, pltpu.roll(got, 120, 1), pltpu.roll(got, 8, 1))
        return got, inner

    mid, top, bottom = pl.ds(G, CY), pl.ds(G + CY, G), pl.ds(0, G)
    own, far = pl.ds(0, CX), pl.ds(CX, CX)
    a, b = side(edge_in[0], edge_in[1], lane)
    field[mid, far] = a
    depth[mid, far] = b
    a, b = side(corner_in[0], corner_in[1], lane8)
    field[top, far] = a * has_north
    depth[top, far] = b * has_north
    a, b = side(corner_in[2], corner_in[3], lane8)
    field[bottom, far] = a * has_south
    depth[bottom, far] = b * has_south
    field[top, own] = rows_in[0, 0] * has_north
    depth[top, own] = rows_in[0, 1] * has_north
    field[bottom, own] = rows_in[1, 0] * has_south
    depth[bottom, own] = rows_in[1, 1] * has_south

    d = depth[...]
    for i, (shift, axis) in enumerate(((COLS - 1, 1), (ROWS - 1, 0))):
        e = pltpu.roll(d, shift, axis)
        wgt[i] = jnp.where((d > 0.0) & (e > 0.0), (STIFFNESS / SPAN * 2.0) * (d + e), 0.0)

    def apply(v):
        fe = wgt[0] * (v - pltpu.roll(v, COLS - 1, 1))
        fn = wgt[1] * (v - pltpu.roll(v, ROWS - 1, 0))
        return (fe - pltpu.roll(fe, 1, 1)) + (fn - pltpu.roll(fn, 1, 0))

    partial = []
    v, before = field[...], None
    for k in range(ITERS):
        image = apply(v)
        if k == 0:
            basis[...] = image
            nxt = 0.5 * image - v
        else:
            nxt = (image - 2.0 * v) - before
        here, there = v[G : G + CY, :CX], nxt[G : G + CY, :CX]
        partial.append(folded(here * here))
        partial.append(folded(here * there))
        v, before = nxt, v
    nm = len(partial)
    hi = jnp.stack([x[0] for x in partial])
    lo = jnp.stack([x[1] for x in partial])
    for s in (4, 2, 1):
        hi, lo = df_add((hi, lo), (pltpu.roll(hi, s, 1), pltpu.roll(lo, s, 1)))
    sub8 = lax.broadcasted_iota(jnp.int32, (8, CX), 0)

    def packed(x):
        done = []
        for first in (0, 8):
            t = jnp.zeros((8, CX), F32)
            for j in range(first, min(first + 8, nm)):
                t = jnp.where(sub8 == j - first, x[j], t)
            done.append(t)
        return jnp.concatenate(done, axis=0)

    hi, lo = packed(hi), packed(lo)
    for s in (64, 32, 16, 8, 4, 2, 1):
        hi, lo = df_add((hi, lo), (pltpu.roll(hi, s, 1), pltpu.roll(lo, s, 1)))
    letter = jnp.where(
        lane8 < 64,
        jnp.where(lane8 < 32, hi[:8], hi[8:]),
        jnp.where(lane8 < 96, lo[:8], lo[8:]),
    )

    def post(st):
        mail[st] = letter
        for i, off in enumerate(peers(STAGES[st])):
            pltpu.make_async_remote_copy(
                mail.at[st], mail_in.at[st, i], mail_sem.at[0, st], mail_sem.at[1, st],
                device_id=peer(STAGES[st], off),
            ).start()

    def collect(st):
        pltpu.make_async_copy(mail_in.at[st], mail_in.at[st], mail_sem.at[1, st]).wait()
        his = [mail[st]] + [mail_in[st, i] for i in range(len(peers(STAGES[st])))]
        terms = [(t, pltpu.roll(t, 64, 1)) for t in his]
        while len(terms) > 1:
            terms = [df_add(terms[i], terms[i + 1]) for i in range(0, len(terms), 2)]
        return terms[0]

    await_ready(2)
    post(0)
    feed(BATCH[4])

    for c in loads[6:]:
        c.wait()
    z = jnp.zeros((CY, CX), F32)
    zn = jnp.zeros((8, CX), F32)
    zs = jnp.zeros((8, CX), F32)
    for k in range(LEV):
        m = lm[k].astype(F32) * ta[k]
        ec = DIFFUSE - 0.5 * ev[k]
        wc = DIFFUSE + 0.5 * ev[k]
        nc = DIFFUSE - 0.5 * nv[k]
        sc = DIFFUSE + 0.5 * nv[k]
        ef, wf, nf, sf = ec * m, wc * m, nc * m, sc * m
        inflow = jnp.where(lane == 0, 0.0, pltpu.roll(ef, 1, 1))
        inflow = inflow + jnp.where(lane == CX - 1, 0.0, pltpu.roll(wf, CX - 1, 1))
        inflow = inflow + jnp.where(row == 0, 0.0, pltpu.roll(nf, 1, 0))
        inflow = inflow + jnp.where(row == CY - 1, 0.0, pltpu.roll(sf, CY - 1, 0))
        back[k] = m + TIMESTEP * (inflow - (ec + wc + nc + sc) * m)
        z = jnp.where(lane == k, pltpu.roll(wf, k, 1) if k else wf, z)
        z = jnp.where(lane == 120 + k, pltpu.roll(ef, 121 + k, 1) if k < 7 else ef, z)
        zrow[1, pl.ds(k, 1)] = nf[CY - 1 :]
        zrow[0, pl.ds(k, 1)] = sf[:1]
    zed[...] = z
    zeds = []
    for i, (a, b, who) in enumerate((
        (zed, zed_in.at[0], (west, gy)),
        (zed, zed_in.at[1], (east, gy)),
        (zrow.at[0], zrow_in.at[0], (gx, south)),
        (zrow.at[1], zrow_in.at[1], (gx, north)),
    )):
        c = pltpu.make_async_remote_copy(a, b, zed_sem.at[0, i], zed_sem.at[1, i], device_id=who)
        c.start()
        zeds.append(c)

    total = collect(0)
    letter = jnp.where(lane8 < 64, total[0], pltpu.roll(total[1], 64, 1))
    post(1)
    feed(LEV)

    total = collect(1)
    cur = tuple(jnp.concatenate([t, pltpu.roll(t, 96, 1)], axis=0) for t in total)
    order = lax.broadcasted_iota(jnp.int32, cur[0].shape, 0)
    later = order >= 2
    base = [jnp.where(later, jnp.where(order % 2 == 0, x[:1], x[1:2]), 0.0) for x in cur]
    cur = df_add([jnp.where(later, 2.0 * x, x) for x in cur], [-x for x in base])
    shrink = jnp.ones(cur[0].shape, F32)
    for k in range(2, 2 * ITERS):
        shrink = jnp.where(order >= k, 0.5 * shrink, shrink)
    cur = (cur[0] * shrink, cur[1] * shrink)
    couple = jnp.where(order == 1, 0.5, 0.25)
    prev = None

    def pick(x, k):
        return x[0][k : k + 1], x[1][k : k + 1]

    def spread(x):
        return jnp.broadcast_to(x[0], cur[0].shape), jnp.broadcast_to(x[1], cur[0].shape)

    def up(x):
        return pltpu.roll(x[0], 15, 0), pltpu.roll(x[1], 15, 0)

    def down(x):
        return couple * pltpu.roll(x[0], 1, 0), couple * pltpu.roll(x[1], 1, 0)

    norm = pick(cur, 0)
    ratio = df_div(pick(cur, 1), norm)
    ja, jb = [ratio], []
    for k in range(1, ITERS):
        nxt = df_add(df_add(up(cur), down(cur)), df_neg(df_mul(spread(ja[-1]), cur)))
        if k > 1:
            nxt = df_add(nxt, df_neg(df_mul(spread(jb[-1]), prev)))
        fresh = pick(nxt, k)
        new_ratio = df_div(pick(nxt, k + 1), fresh)
        ja.append(df_add(new_ratio, df_neg(ratio)))
        jb.append(df_div(fresh, norm))
        norm, ratio, prev, cur = fresh, new_ratio, cur, nxt
    steps, growths = [], []
    for k in range(ITERS):
        diag = 1.0 + (SPAN / 2.0) * ((1.0 + ja[k][0]) + ja[k][1])
        if k:
            off = (SPAN * SPAN / 4.0) * (jb[k - 1][0] + jb[k - 1][1])
            growths.append(off * steps[-1] * steps[-1])
            diag = diag - off * steps[-1]
        steps.append(1.0 / diag)
    whole = (ROWS, COLS)
    steps = [jnp.broadcast_to(x[:1, :1], whole) for x in steps]
    growths = [jnp.broadcast_to(x[:1, :1], whole) for x in growths]

    r = field[...]
    p = r
    s = jnp.zeros_like(r)
    for k in range(ITERS):
        s = s + steps[k] * p
        if k + 1 < ITERS:
            q = p + (SPAN / 4.0) * (basis[...] if k == 0 else apply(p))
            r = r - steps[k] * q
            p = r + growths[k] * p
    load = depth[...] * s
    flow_e = jnp.where(wgt[0] > 0.0, pltpu.roll(load, COLS - 1, 1) - load, 0.0)
    flow_n = jnp.where(wgt[1] > 0.0, pltpu.roll(load, ROWS - 1, 0) - load, 0.0)
    pull = (flow_e - pltpu.roll(flow_e, 1, 1)) + (flow_n - pltpu.roll(flow_n, 1, 0))
    sol[...] = s[G : G + CY, :CX]
    pressure = -GRAVITY * pull[G : G + CY, :CX]
    for c in zeds:
        c.wait_recv()
    ze, zw = zed_in[0], zed_in[1]
    for k in range(LEV):
        b = back[k]
        b = b + jnp.where(lane == 0, pltpu.roll(zw, 8 - k, 1), 0.0)
        b = b + jnp.where(lane == CX - 1, pltpu.roll(ze, 127 - k, 1), 0.0)
        b = b + jnp.where(row == 0, zrow_in[1, pl.ds(k, 1)] * has_south, 0.0)
        b = b + jnp.where(row == CY - 1, zrow_in[0, pl.ds(k, 1)] * has_north, 0.0)
        dens = ((1.0 + k / LEV) * pressure) * lm[k].astype(F32)
        bulks[k].wait_recv()
        ct, cs = fetched[0, k], fetched[1, k]
        out[0, k] = b + (THERMAL + 2.0 * NONLINEAR * ct + CABBELING * cs) * dens
        out[1, k] = (HALINE + CABBELING * ct) * dens
    for c in halos + bulks + zeds:
        c.wait_send()
    for st in range(2):
        pltpu.make_async_copy(mail_in.at[st], mail_in.at[st], mail_sem.at[0, st]).wait()


def deliver(both, sol, tb_h, sb_h, sa_h, sem):
    copies = [
        pltpu.make_async_copy(a, b, sem.at[i])
        for i, (a, b) in enumerate(((both.at[0], tb_h), (both.at[1], sb_h), (sol, sa_h)))
    ]
    for c in copies:
        c.start()
    for c in copies:
        c.wait()


def body(ta, ha, ev, nv, ts, ss, slots, lm, od):
    vm = lambda *shape: pltpu.VMEM(shape, F32)
    cube = (LEV, CY, CX)
    dma = lambda *shape: pltpu.SemaphoreType.DMA(shape)
    n = len(peers(STAGES[0]))
    hbm = pl.BlockSpec(memory_space=pltpu.HBM)
    vmem = pl.BlockSpec(memory_space=pltpu.VMEM)
    both, sol = pl.pallas_call(
        kernel,
        out_shape=(jax.ShapeDtypeStruct((2,) + cube, F32), jax.ShapeDtypeStruct((CY, CX), F32)),
        in_specs=[hbm] * 9,
        out_specs=(vmem, vmem),
        scratch_shapes=[
            vm(*cube), vm(CY, CX), vm(*cube), vm(*cube), vm(2, *cube), pltpu.VMEM(cube, jnp.int32), vm(CY, CX),
            pltpu.SMEM((1, 1, LEV), jnp.int32),
            vm(2, *cube), vm(2, *cube), vm(*cube),
            vm(CY, CX), vm(2, CY, CX), vm(2, 2, 8, CX), vm(2, 2, 8, CX), vm(4, 8, CX),
            vm(CY, CX), vm(2, CY, CX), vm(2, 8, CX), vm(2, 8, CX),
            vm(ROWS, COLS), vm(ROWS, COLS), vm(2, ROWS, COLS), vm(ROWS, COLS),
            vm(2, 8, CX), vm(2, n, 8, CX),
            dma(10), dma(2, LEV), dma(2, 8), dma(2, 4), dma(2, 2), pltpu.SemaphoreType.REGULAR((2, 2)),
        ],
        compiler_params=pltpu.CompilerParams(
            collective_id=0, has_side_effects=True, vmem_limit_bytes=40 << 20
        ),
        cost_estimate=pl.CostEstimate(flops=40000000, bytes_accessed=60000000, transcendentals=0),
        name="adjoint",
    )(*[pltpu.with_memory_space_constraint(x, pltpu.HBM) for x in (slots, ta, ha, ev, nv, ts, ss, lm, od)])
    return pl.pallas_call(
        deliver,
        out_shape=(
            jax.ShapeDtypeStruct(cube, F32),
            jax.ShapeDtypeStruct(cube, F32),
            jax.ShapeDtypeStruct((CY, CX), F32),
        ),
        in_specs=[vmem, vmem],
        out_specs=(hbm, hbm, hbm),
        scratch_shapes=[dma(3)],
        name="deliver",
    )(*[pltpu.with_memory_space_constraint(x, pltpu.VMEM) for x in (both, sol)])


def solution(mesh):
    cube, flat = P(None, "gy", "gx"), P("gy", "gx")
    return jax.shard_map(
        body,
        mesh=mesh,
        in_specs=(cube, flat, cube, cube, cube, cube, P("gx", "gy", None), cube, flat),
        out_specs=(cube, cube, flat),
        check_vma=False,
    )
```
